32 devices in a mesh: hor: 4 (over y, core), lat: 8 (over z, x).
Axes of the slice: x: 2, y: 2, z: 4, core: 2. Of those that a mesh axis runs over, the one named last changes fastest.
Arguments:
- window: float32 [4, 69, 64, 128], P('hor', None, 'lat'), may hold values from -6 to 6
- fresh_noise: float32 [69, 64, 128], P(None, 'lat'), may hold values from -6 to 6
- level_index: int32 [4], P('hor'), may hold values from 4 to 63
- plan: float32 [64], replicated, may hold values from 0.07 to 38.42, as said below
- retention: float32 [4, 192], P('hor'), may hold values from 0.12 to 1
- lift_weight: bfloat16 [192, 69], replicated, may hold values from -0.75 to 0.75
- mod_scale: float32 [192], replicated, may hold values from -3 to 3
- mod_shift: float32 [192], replicated, may hold values from -3 to 3
- conv_weight: bfloat16 [3, 192, 576], replicated, may hold values from -0.15625 to 0.15625
- out_weight: bfloat16 [69, 192], replicated, may hold values from -0.4375 to 0.4375
Outputs:
- window_out: float32 [4, 69, 64, 128], P('hor', None, 'lat')
- rolled: float32 [4, 69, 64, 128], P('hor', None, 'lat')
The draws below stay inside these ranges and needn't reach their ends.
Inputs may be any that keep to these rules, and one draw needn't show every extreme that they name: `plan`: rising from each entry to the next.
All inputs are finite; a program needn't handle non-finite values.
Results may differ from the reference program's by a relative error of at most 0.00064.
Values may be sent and summed in bfloat16 or wider, within the bound.
A program may use at most 64 MiB of HBM per device.

```python
import jax
import jax.numpy as jnp
from jax import lax

C = 69
HIDDEN_CHANNELS = 192
LON = 128
POOL = 4
STEPS = 3
LEVELS = 64
LEAD_FRAMES = 4
LAT = 64


def draw_level_index(key, part):
    span_size = max(1, (LEVELS - STEPS - 2) // LEAD_FRAMES)
    base_level = STEPS + 1 + jnp.arange(LEAD_FRAMES, dtype=jnp.int32) * (LEVELS - STEPS - 2) // LEAD_FRAMES
    offsets = jax.random.randint(jax.random.fold_in(key, 3), (LEAD_FRAMES,), 0, span_size, dtype=jnp.int32)
    levels = jnp.minimum(base_level + offsets, LEVELS - 1)
    levels = levels.at[0].set(STEPS + 1).at[LEAD_FRAMES - 1].set(LEVELS - 1)
    return levels.astype(jnp.int32)


def draw_plan(key, part):
    key_inc = jax.random.fold_in(key, 5)
    steps_up = jax.random.uniform(key_inc, (LEVELS,), jnp.float32, 0.05, 0.6)
    return (0.02 + jnp.cumsum(steps_up)).astype(jnp.float32)


def draw_retention(key, part):
    key_mask = jax.random.fold_in(key, 7)
    key_fast = jax.random.fold_in(key, 8)
    key_slow = jax.random.fold_in(key, 9)
    spike_key = jax.random.fold_in(key, 10)
    depth_key = jax.random.fold_in(key, 12)
    slow_share = 0.5
    slow_mask = jax.random.uniform(key_mask, (HIDDEN_CHANNELS,)) < slow_share
    fast_rate = jax.random.uniform(key_fast, (LEAD_FRAMES, HIDDEN_CHANNELS), jnp.float32, 0.25, 0.6)
    slow_rate = 1.0 - jax.random.uniform(key_slow, (LEAD_FRAMES, HIDDEN_CHANNELS), jnp.float32, 0.2, 1.0) / LEAD_FRAMES
    baseline_rate = jnp.where(slow_mask[None, :], slow_rate, fast_rate)
    spike_frames = jax.random.randint(spike_key, (2,), 0, LEAD_FRAMES, dtype=jnp.int32)
    struck_frame = jnp.any(jnp.arange(LEAD_FRAMES, dtype=jnp.int32)[:, None] == spike_frames[None, :], axis=1)
    spike_depth = jax.random.uniform(depth_key, (HIDDEN_CHANNELS,), jnp.float32, 0.5, 0.8)
    frame_rates = jnp.where(struck_frame[:, None], baseline_rate * spike_depth[None, :], baseline_rate)
    return frame_rates.astype(jnp.float32)


def block_levels(own_key, shape, pieces, low, high):
    def one(dim, blocks):
        heights = jax.random.uniform(jax.random.fold_in(jax.random.fold_in(own_key, 6), dim), (blocks,), jnp.float32, low / len(pieces), high / len(pieces))
        return jnp.repeat(jnp.exp(heights), shape[dim] // blocks).reshape((-1,) + (1,) * (len(shape) - dim - 1))

    gain = one(*pieces[0])
    for cut in pieces[1:]:
        gain = gain * one(*cut)
    return gain


def scatter_about(stream_key, shape, scale, limit, cuts=(), kind=jnp.bfloat16):
    gain = block_levels(stream_key, shape, cuts, -0.22, 0.18) if cuts else 1.0
    array = jax.random.normal(stream_key, shape, jnp.float32) * scale * gain
    return jnp.minimum(jnp.maximum(array, -limit), limit).astype(kind)


def setup_inputs(seed: int = 0) -> dict:
    seeds = jax.random.split(jax.random.key(seed), 11)
    window = scatter_about(seeds[0], (LEAD_FRAMES, C, LAT, LON), 1.0, 6.0, ((0, 4), (2, 8)), jnp.float32)
    fresh_noise = scatter_about(seeds[1], (C, LAT, LON), 1.0, 6.0, ((1, 8),), jnp.float32)
    level_index = draw_level_index(jax.random.fold_in(seeds[10], 71), 0)
    plan = draw_plan(jax.random.fold_in(seeds[10], 71), 0)
    retention = draw_retention(jax.random.fold_in(seeds[10], 71), 0)
    lift_weight = scatter_about(seeds[5], (HIDDEN_CHANNELS, C), C ** -0.5, 0.75)
    mod_scale = scatter_about(seeds[6], (HIDDEN_CHANNELS,), 0.3, 3.0, (), jnp.float32)
    mod_shift = scatter_about(seeds[7], (HIDDEN_CHANNELS,), 0.5, 3.0, (), jnp.float32)
    conv_weight = scatter_about(seeds[8], (3, HIDDEN_CHANNELS, 3 * HIDDEN_CHANNELS), (9 * HIDDEN_CHANNELS) ** -0.5, 0.15625)
    out_weight = scatter_about(seeds[9], (C, HIDDEN_CHANNELS), HIDDEN_CHANNELS ** -0.5, 0.4375)
    return dict(window=window, fresh_noise=fresh_noise, level_index=level_index, plan=plan, retention=retention, lift_weight=lift_weight, mod_scale=mod_scale, mod_shift=mod_shift, conv_weight=conv_weight, out_weight=out_weight)


def lookup(sched_table, level_at):
    levels = jnp.arange(sched_table.shape[0], dtype=jnp.int32)
    onehot = (level_at[:, None] == levels[None, :]).astype(jnp.float32)
    return lax.optimization_barrier(jnp.sum(onehot * sched_table[None, :], axis=1))

def lift_frame(frame_in, scale_mod, shift_mod, lift_weight):
    lifted = jnp.einsum('dc,clw->dlw', lift_weight.astype(jnp.float32), frame_in.astype(jnp.float32))
    return jax.nn.silu(lifted * scale_mod[:, None, None] + shift_mod[:, None, None]).astype(jnp.bfloat16)

def pool_cells(features):
    hidden, lat_rows, lon_cells = features.shape
    blocks = features.astype(jnp.float32).reshape(hidden, lat_rows // POOL, POOL, lon_cells // POOL, POOL)
    return lax.optimization_barrier(jnp.mean(blocks, axis=(2, 4))).reshape(hidden, -1)

def upsample(context, lat_rows, lon_cells):
    hidden = context.shape[0]
    coarse = context.reshape(hidden, lat_rows // POOL, 1, lon_cells // POOL, 1)
    spread_ctx = jnp.broadcast_to(coarse, (hidden, lat_rows // POOL, POOL, lon_cells // POOL, POOL))
    return spread_ctx.reshape(hidden, lat_rows, lon_cells)

def conv_frame(features, conv_weight):
    lat_rows = features.shape[1]
    padded = jnp.pad(features, ((0, 0), (1, 1), (0, 0)))
    conv_sum = jnp.zeros((conv_weight.shape[1],) + features.shape[1:], jnp.float32)
    for row_off in range(3):
        row_slab = padded[:, row_off:row_off + lat_rows, :]
        stacked = jnp.concatenate([jnp.roll(row_slab, 1 - col_off, axis=2) for col_off in range(3)], axis=0)
        conv_sum = conv_sum + jnp.einsum('dk,klw->dlw', conv_weight[row_off].astype(jnp.float32), stacked.astype(jnp.float32))
    return conv_sum

def finish_frame(features, context, conv_weight, out_weight):
    conv_sum = conv_frame(features, conv_weight)
    mixed_sum = features.astype(jnp.float32) + conv_sum + upsample(context, features.shape[1], features.shape[2])
    gated_out = jax.nn.silu(mixed_sum).astype(jnp.bfloat16)
    return jnp.einsum('cd,dlw->clw', out_weight.astype(jnp.float32), gated_out.astype(jnp.float32))

def reference(window, fresh_noise, level_index, plan, retention, lift_weight, mod_scale, mod_shift, conv_weight, out_weight):
    current = window
    for section in range(STEPS):
        sigma_now = lookup(plan, level_index - section)
        sigma_next = lookup(plan, level_index - section - 1)
        in_scale = 1.0 / jnp.sqrt(sigma_now * sigma_now + 1.0)
        scaled = (current * in_scale[:, None, None, None]).astype(jnp.bfloat16)
        log_sigma = jnp.log(sigma_now)
        scale_mod = 1.0 + log_sigma[:, None] * mod_scale[None, :]
        shift_mod = log_sigma[:, None] * mod_shift[None, :]
        features = lax.map(lambda packed: lift_frame(packed[0], packed[1], packed[2], lift_weight), (scaled, scale_mod, shift_mod))
        pooled = lax.map(pool_cells, features)

        def carry_step(running, packed):
            running = packed[0][:, None] * running + packed[1]
            return (running, running)
        _, context = lax.scan(carry_step, jnp.zeros(pooled.shape[1:], jnp.float32), (retention, pooled))
        outputs = lax.map(lambda packed: finish_frame(packed[0], packed[1], conv_weight, out_weight), (features, context))
        skip_scale = 1.0 / (sigma_now * sigma_now + 1.0)
        out_scale = sigma_now * in_scale
        denoised = skip_scale[:, None, None, None] * current + out_scale[:, None, None, None] * outputs
        current = denoised + (sigma_next / sigma_now)[:, None, None, None] * (current - denoised)
    top_sigma = plan[LEVELS - 1]
    rolled = jnp.concatenate([current[1:], (top_sigma * fresh_noise)[None]], axis=0)
    return (current, rolled)
```

```python
import functools

import jax
import jax.numpy as jnp
from jax import lax
from jax.experimental import pallas as pl
from jax.experimental.pallas import tpu as pltpu
from jax.sharding import PartitionSpec as P

POOL = 4
STEPS = 3
MESH = pl.DeviceIdType.MESH
F32 = jnp.float32
BF16 = jnp.bfloat16
WIRE = jnp.bfloat16


def dot(a, b):
    return jnp.dot(a, b, preferred_element_type=F32)


def silu(x):
    h = 0.5 * x
    return h + h * jnp.tanh(h)


def kernel(
    rows,
    lon,
    n_hor,
    n_lat,
    lvl,
    plan,
    win,
    ret,
    msc,
    msh,
    liftw,
    convw,
    outw,
    wout,
    arr,
    cur,
    stack,
    acc,
    up,
    coef,
    mods,
    poolm,
    spread,
    ctx,
    hsend,
    hrecv,
    psend,
    precv,
    rrecv,
    h_ssem,
    h_rsem,
    p_ssem,
    p_rsem,
    r_ssem,
    r_rsem,
    f_sem,
):
    hidden, chans = liftw.shape
    half = hidden // 2
    pair = 2 * lon
    n_pairs = rows // 2
    hor = lax.axis_index("hor")
    lat = lax.axis_index("lat")

    barrier = pltpu.get_barrier_semaphore()

    @pl.when(lat > 0)
    def _():
        pl.semaphore_signal(barrier, inc=1, device_id={"lat": lat - 1}, device_id_type=MESH)

    @pl.when(lat < n_lat - 1)
    def _():
        pl.semaphore_signal(barrier, inc=1, device_id={"lat": lat + 1}, device_id_type=MESH)

    for d in range(1, n_hor):
        pl.semaphore_signal(
            barrier, inc=1, device_id={"hor": lax.rem(hor + d, n_hor)}, device_id_type=MESH
        )

    for row in range(rows):
        cur[:, row * lon : (row + 1) * lon] = win[pl.ds(row, chans, stride=rows), :]

    def column(row_ref_value, start, count):
        sub = lax.broadcasted_iota(jnp.int32, (count, hidden), 0) + start
        lane = lax.broadcasted_iota(jnp.int32, (count, hidden), 1)
        return jnp.sum(jnp.where(sub == lane, row_ref_value, 0.0), axis=1, keepdims=True)

    mods[0] = jnp.broadcast_to(column(msc[...], 0, hidden), (hidden, lon))
    mods[1] = jnp.broadcast_to(column(msh[...], 0, hidden), (hidden, lon))

    def packed_rate(value):
        lane = lax.broadcasted_iota(jnp.int32, (half, lon), 1)
        lo = jnp.broadcast_to(column(value, 0, half), (half, lon))
        hi = jnp.broadcast_to(column(value, half, half), (half, lon))
        return jnp.where(lane < lon // 2, lo, hi)

    groups = lon // POOL
    for tok in range(rows // POOL):
        for side in range(2):
            k = lax.broadcasted_iota(jnp.int32, (pair, lon), 0)
            n = lax.broadcasted_iota(jnp.int32, (pair, lon), 1)
            want = side * (lon // 2) + tok * groups + lax.shift_right_logical(
                lax.bitwise_and(k, lon - 1), POOL.bit_length() - 1
            )
            poolm[2 * tok + side] = jnp.where(want == n, 1.0 / (POOL * POOL), 0.0).astype(BF16)
    for side in range(2):
        k = lax.broadcasted_iota(jnp.int32, (2 * lon, pair), 0)
        n = lax.broadcasted_iota(jnp.int32, (2 * lon, pair), 1)
        want = side * (lon // 2) + lax.shift_right_logical(n, POOL.bit_length() - 1)
        spread[side] = jnp.where(lax.bitwise_and(k, lon - 1) == want, 1.0, 0.0).astype(BF16)

    def sigma(s, width):
        at = lvl[0] - s
        now = jnp.full((1, width), plan[jnp.maximum(at, 0)], F32)
        after = jnp.full((1, width), plan[jnp.maximum(at - 1, 0)], F32)
        return now, after

    def in_scale_of(now):
        return 1.0 / jnp.sqrt(now * now + 1.0)

    def halo_copy(s, side):
        return pltpu.make_async_remote_copy(
            src_ref=hsend.at[s, side],
            dst_ref=hrecv.at[s, 1 - side],
            send_sem=h_ssem.at[s, side],
            recv_sem=h_rsem.at[s, 1 - side],
            device_id={"lat": lat - 1 if side == 0 else lat + 1},
            device_id_type=MESH,
        )

    def has(side):
        return lat > 0 if side == 0 else lat < n_lat - 1

    def stage_halo(s):
        scale = in_scale_of(sigma(s, lon)[0])
        for side in range(2):
            at = 0 if side == 0 else (rows - 1) * lon
            hsend[s, side, 0:chans, :] = (cur[:, at : at + lon] * scale).astype(BF16)

    def send_halo(s):
        for side in range(2):

            @pl.when(has(side))
            def _():
                halo_copy(s, side).start()

    def pool_copy(s, d):
        return pltpu.make_async_remote_copy(
            src_ref=psend.at[s],
            dst_ref=precv.at[s, d - 1],
            send_sem=p_ssem.at[s, d - 1],
            recv_sem=p_rsem.at[s, d - 1],
            device_id={"hor": hor + d},
            device_id_type=MESH,
        )

    def rate_copy(d):
        return pltpu.make_async_remote_copy(
            src_ref=ret,
            dst_ref=rrecv.at[d - 1],
            send_sem=r_ssem.at[d - 1],
            recv_sem=r_rsem.at[d - 1],
            device_id={"hor": hor + d},
            device_id_type=MESH,
        )

    def lift(scaled, sm, sh):
        return silu(dot(liftw[...], scaled) * sm + sh).astype(F32)

    def place(feat, block):
        at = block * lon
        low = feat.astype(BF16)
        stack[0:hidden, at : at + lon] = pltpu.roll(feat, 1, 1).astype(BF16)
        stack[hidden : 2 * hidden, at : at + lon] = low
        stack[2 * hidden : 3 * hidden, at : at + lon] = pltpu.roll(feat, lon - 1, 1).astype(BF16)

    stage_halo(0)
    n_near = jnp.where(lat > 0, 1, 0) + jnp.where(lat < n_lat - 1, 1, 0)
    pl.semaphore_wait(barrier, n_near + (n_hor - 1))
    send_halo(0)
    for d in range(1, n_hor):

        @pl.when(hor + d < n_hor)
        def _():
            rate_copy(d).start()

    @pl.loop(0, STEPS)
    def _(s):
        now, after = sigma(s, lon)
        scale = in_scale_of(now)
        log_sigma = jnp.log(now)
        sm = 1.0 + log_sigma * mods[0]
        sh = log_sigma * mods[1]
        for p in range(n_pairs):
            scaled = jnp.concatenate(
                [
                    (cur[:, (2 * p + i) * lon : (2 * p + i + 1) * lon] * scale).astype(BF16)
                    for i in range(2)
                ],
                axis=1,
            )
            lifted = dot(liftw[...], scaled)
            for i in range(2):
                place(silu(lifted[:, i * lon : (i + 1) * lon] * sm + sh), 2 * p + i + 1)
        pooled = jnp.zeros((half, lon), F32)
        for p in range(n_pairs):
            tok = 2 * p // POOL
            for side in range(2):
                k0 = hidden + side * half
                feat = stack[k0 : k0 + half, (2 * p + 1) * lon : (2 * p + 3) * lon]
                pooled = pooled + dot(feat, poolm[2 * tok + side])
        psend[s] = pooled.astype(WIRE)
        for d in range(1, n_hor):

            @pl.when(hor + d < n_hor)
            def _():
                pool_copy(s, d).start()

        ctx[...] = pooled
        for p in range(n_pairs):
            total = dot(convw[1], stack[:, (2 * p + 1) * lon : (2 * p + 3) * lon])
            if p > 0:
                total = total + dot(convw[0], stack[:, 2 * p * lon : (2 * p + 2) * lon])
            if p < n_pairs - 1:
                total = total + dot(convw[2], stack[:, (2 * p + 2) * lon : (2 * p + 4) * lon])
            acc[:, p * pair : (p + 1) * pair] = total
        acc[:, lon:pair] += dot(convw[0], stack[:, lon:pair])
        last = (rows - 1) * lon
        acc[:, last - lon : last] += dot(convw[2], stack[:, rows * lon : (rows + 1) * lon])

        for side in range(2):

            @pl.when(has(side))
            def _():
                halo_copy(s, 1 - side).wait_recv()
                feat = silu(dot(liftw[...], hrecv[s, side, 0:chans, :]) * sm + sh)
                block = 0 if side == 0 else rows + 1
                place(feat, block)
                at = 0 if side == 0 else last
                acc[:, at : at + lon] += dot(
                    convw[2 * side], stack[:, block * lon : (block + 1) * lon]
                )

        @pl.when(s == 0)
        def _():
            coef[0] = packed_rate(ret[...])
            for d in range(1, n_hor):

                @pl.when(hor >= d)
                def _():
                    rate_copy(d).wait_recv()
                    if d < n_hor - 1:
                        coef[d] = coef[d - 1] * packed_rate(rrecv[d - 1])

        for d in range(1, n_hor):

            @pl.when(hor >= d)
            def _():
                pool_copy(s, d).wait_recv()
                ctx[...] += coef[d - 1] * precv[s, d - 1].astype(F32)

        total = ctx[...]
        high = total.astype(BF16)
        low = (total - high.astype(F32)).astype(BF16)
        both = jnp.concatenate([high, low], axis=1)
        up[0:half, :] = dot(both, spread[0])
        up[half:hidden, :] = dot(both, spread[1])

        ratio = after / now
        keep = ratio + (1.0 - ratio) / (now * now + 1.0)
        gain = (1.0 - ratio) * (now * scale)
        order = [0, n_pairs - 1] + list(range(1, n_pairs - 1))
        for p in order:
            tok = 2 * p // POOL
            ctx_up = up[:, tok * lon : (tok + 1) * lon]
            gated = []
            for i in range(2):
                at = (2 * p + i) * lon
                feat = stack[hidden : 2 * hidden, at + lon : at + 2 * lon].astype(F32)
                gated.append(silu(feat + acc[:, at : at + lon] + ctx_up).astype(BF16))
            outputs = dot(outw[...], jnp.concatenate(gated, axis=1))
            for i in range(2):
                at = (2 * p + i) * lon
                cur[:, at : at + lon] = (
                    keep * cur[:, at : at + lon] + gain * outputs[:, i * lon : (i + 1) * lon]
                )
            if p == order[1]:

                @pl.when(s < STEPS - 1)
                def _():
                    stage_halo(s + 1)
                    send_halo(s + 1)

    for row in range(rows):
        wout[pl.ds(row, chans, stride=rows), :] = cur[:, row * lon : (row + 1) * lon]
    final = pltpu.make_async_remote_copy(
        src_ref=wout,
        dst_ref=arr,
        send_sem=f_sem.at[0],
        recv_sem=f_sem.at[1],
        device_id={"hor": hor - 1},
        device_id_type=MESH,
    )

    @pl.when(hor > 0)
    def _():
        final.start()

    for d in range(1, n_hor):

        @pl.when(hor + d < n_hor)
        def _():
            rate_copy(d).wait_send()
            for s in range(STEPS):
                pool_copy(s, d).wait_send()

    for s in range(STEPS):
        for side in range(2):

            @pl.when(has(side))
            def _():
                halo_copy(s, side).wait_send()

    @pl.when(hor > 0)
    def _():
        final.wait_send()

    @pl.when(hor < n_hor - 1)
    def _():
        final.wait_recv()


def body(
    n_hor,
    n_lat,
    window,
    fresh_noise,
    level_index,
    plan,
    retention,
    lift_weight,
    mod_scale,
    mod_shift,
    conv_weight,
    out_weight,
):
    frames, chans, rows, lon = window.shape
    hidden = conv_weight.shape[1]
    half = hidden // 2
    cells = rows * lon
    cpad = -(-chans // 16) * 16
    peers = max(1, n_hor - 1)
    vmem = pl.BlockSpec(memory_space=pltpu.VMEM)
    smem = pl.BlockSpec(memory_space=pltpu.SMEM)
    flat = jax.ShapeDtypeStruct((chans * rows, lon), F32)
    dma = pltpu.SemaphoreType.DMA
    current, arriving = pl.pallas_call(
        functools.partial(kernel, rows, lon, n_hor, n_lat),
        out_shape=(flat, flat),
        in_specs=[smem, smem] + [vmem] * 7,
        out_specs=(vmem, vmem),
        scratch_shapes=[
            pltpu.VMEM((chans, cells), F32),
            pltpu.VMEM((3 * hidden, cells + 2 * lon), BF16),
            pltpu.VMEM((hidden, cells), F32),
            pltpu.VMEM((hidden, 2 * lon), F32),
            pltpu.VMEM((peers, half, lon), F32),
            pltpu.VMEM((2, hidden, lon), F32),
            pltpu.VMEM((2 * (rows // POOL), 2 * lon, lon), BF16),
            pltpu.VMEM((2, 2 * lon, 2 * lon), BF16),
            pltpu.VMEM((half, lon), F32),
            pltpu.VMEM((STEPS, 2, cpad, lon), BF16),
            pltpu.VMEM((STEPS, 2, cpad, lon), BF16),
            pltpu.VMEM((STEPS, half, lon), WIRE),
            pltpu.VMEM((STEPS, peers, half, lon), WIRE),
            pltpu.VMEM((peers, 1, hidden), F32),
            dma((STEPS, 2)),
            dma((STEPS, 2)),
            dma((STEPS, peers)),
            dma((STEPS, peers)),
            dma((peers,)),
            dma((peers,)),
            dma((2,)),
        ],
        compiler_params=pltpu.CompilerParams(
            collective_id=0, has_side_effects=True, vmem_limit_bytes=40 * 1024 * 1024
        ),
    )(
        level_index,
        plan,
        window.reshape(chans * rows, lon),
        retention,
        mod_scale.reshape(1, hidden),
        mod_shift.reshape(1, hidden),
        lift_weight,
        conv_weight,
        out_weight,
    )
    shape = (frames, chans, rows, lon)
    top = plan[plan.shape[0] - 1]
    last = lax.axis_index("hor") == n_hor - 1
    rolled = jnp.where(last, top * fresh_noise[None], arriving.reshape(shape))
    return (current.reshape(shape), rolled)


def solution(mesh):
    in_specs = (
        P("hor", None, "lat", None),
        P(None, "lat", None),
        P("hor"),
        P(),
        P("hor", None),
        P(),
        P(),
        P(),
        P(),
        P(),
    )
    out_specs = (P("hor", None, "lat", None), P("hor", None, "lat", None))
    run = functools.partial(body, mesh.shape["hor"], mesh.shape["lat"])
    return jax.shard_map(run, mesh=mesh, in_specs=in_specs, out_specs=out_specs, check_vma=False)
```

```python
import functools

import jax
import jax.numpy as jnp
from jax import lax
from jax.experimental import pallas as pl
from jax.experimental.pallas import tpu as pltpu
from jax.sharding import PartitionSpec as P

POOL = 4
STEPS = 3
MESH = pl.DeviceIdType.MESH
F32 = jnp.float32
BF16 = jnp.bfloat16
WIRE = jnp.bfloat16


def dot(a, b):
    return jnp.dot(a, b, preferred_element_type=F32)


def silu(x):
    h = 0.5 * x
    return h + h * jnp.tanh(h)


def kernel(
    rows,
    lon,
    n_hor,
    n_lat,
    lvl,
    plan,
    win_h,
    fresh_h,
    ret_h,
    msc_h,
    msh_h,
    lift_h,
    convw_h,
    outw_h,
    wout,
    arr,
    win,
    ret,
    msc,
    msh,
    liftt,
    convw,
    outw,
    liftw,
    base_send,
    base_recv,
    gain_send,
    gain_recv,
    cur,
    stack,
    acc,
    up,
    coef,
    mods,
    poolm,
    spread,
    ctx,
    hsend,
    hrecv,
    psend,
    precv,
    rrecv,
    h_ssem,
    h_rsem,
    p_ssem,
    p_rsem,
    r_ssem,
    r_rsem,
    l_sem,
    f_sem,
    g_ssem,
    g_rsem,
):
    hidden, chans = liftw.shape
    half = hidden // 2
    pair = 2 * lon
    n_pairs = rows // 2
    hor = lax.axis_index("hor")
    lat = lax.axis_index("lat")

    barrier = pltpu.get_barrier_semaphore()

    @pl.when(lat > 0)
    def _():
        pl.semaphore_signal(barrier, inc=1, device_id={"lat": lat - 1}, device_id_type=MESH)

    @pl.when(lat < n_lat - 1)
    def _():
        pl.semaphore_signal(barrier, inc=1, device_id={"lat": lat + 1}, device_id_type=MESH)

    for d in range(1, n_hor):
        pl.semaphore_signal(
            barrier, inc=1, device_id={"hor": lax.rem(hor + d, n_hor)}, device_id_type=MESH
        )

    pairs = [(win_h, win), (msc_h, msc), (msh_h, msh), (ret_h, ret), (lift_h, liftt)]
    pairs += [(convw_h, convw), (outw_h, outw)]
    loads = [pltpu.make_async_copy(a, b, l_sem.at[i]) for i, (a, b) in enumerate(pairs)]
    fresh_load = pltpu.make_async_copy(fresh_h, arr, l_sem.at[len(pairs)])
    for load in loads:
        load.start()

    @pl.when(hor == n_hor - 1)
    def _():
        fresh_load.start()

    for side in range(2):

        @pl.when(jnp.logical_not(lat > 0 if side == 0 else lat < n_lat - 1))
        def _():
            hrecv[:, side] = jnp.zeros_like(hrecv[:, side])

    def column(row_ref_value, start, count):
        sub = lax.broadcasted_iota(jnp.int32, (count, hidden), 0) + start
        lane = lax.broadcasted_iota(jnp.int32, (count, hidden), 1)
        return jnp.sum(jnp.where(sub == lane, row_ref_value, 0.0), axis=1, keepdims=True)

    def packed_rate(value):
        lane = lax.broadcasted_iota(jnp.int32, (half, lon), 1)
        lo = jnp.broadcast_to(column(value, 0, half), (half, lon))
        hi = jnp.broadcast_to(column(value, half, half), (half, lon))
        return jnp.where(lane < lon // 2, lo, hi)

    groups = lon // POOL
    for tok in range(rows // POOL):
        for side in range(2):
            k = lax.broadcasted_iota(jnp.int32, (pair, lon), 0)
            n = lax.broadcasted_iota(jnp.int32, (pair, lon), 1)
            want = side * (lon // 2) + tok * groups + lax.shift_right_logical(
                lax.bitwise_and(k, lon - 1), POOL.bit_length() - 1
            )
            poolm[2 * tok + side] = jnp.where(want == n, 1.0 / (POOL * POOL), 0.0).astype(BF16)
    for side in range(2):
        k = lax.broadcasted_iota(jnp.int32, (2 * lon, pair), 0)
        n = lax.broadcasted_iota(jnp.int32, (2 * lon, pair), 1)
        want = side * (lon // 2) + lax.shift_right_logical(n, POOL.bit_length() - 1)
        spread[side] = jnp.where(lax.bitwise_and(k, lon - 1) == want, 1.0, 0.0).astype(BF16)

    def sigma(s, width):
        at = lvl[0] - s
        now = jnp.full((1, width), plan[jnp.maximum(at, 0)], F32)
        after = jnp.full((1, width), plan[jnp.maximum(at - 1, 0)], F32)
        return now, after

    def in_scale_of(now):
        return 1.0 / jnp.sqrt(now * now + 1.0)

    def halo_copy(s, side):
        return pltpu.make_async_remote_copy(
            src_ref=hsend.at[s, side],
            dst_ref=hrecv.at[s, 1 - side],
            send_sem=h_ssem.at[s, side],
            recv_sem=h_rsem.at[s, 1 - side],
            device_id={"lat": lat - 1 if side == 0 else lat + 1},
            device_id_type=MESH,
        )

    def has(side):
        return lat > 0 if side == 0 else lat < n_lat - 1

    def stage_halo(s, side):
        scale = in_scale_of(sigma(s, lon)[0])
        at = 0 if side == 0 else (rows - 1) * lon
        hsend[s, side, 0:chans, :] = (cur[:, at : at + lon] * scale).astype(BF16)

    def send_halo(s, side):
        @pl.when(has(side))
        def _():
            halo_copy(s, side).start()

    base_copy = pltpu.make_async_remote_copy(
        src_ref=base_send,
        dst_ref=base_recv,
        send_sem=f_sem.at[0],
        recv_sem=f_sem.at[1],
        device_id={"hor": hor - 1},
        device_id_type=MESH,
    )
    units = [[0], [rows - 1]] + [[r, r + 1] for r in range(1, rows - 1, 2)]

    def gain_copy(u):
        part = pl.ds(units[u][0] * lon, len(units[u]) * lon)
        return pltpu.make_async_remote_copy(
            src_ref=gain_send.at[:, part],
            dst_ref=gain_recv.at[:, part],
            send_sem=g_ssem.at[u],
            recv_sem=g_rsem.at[u],
            device_id={"hor": hor - 1},
            device_id_type=MESH,
        )

    def pool_copy(s, d):
        return pltpu.make_async_remote_copy(
            src_ref=psend.at[s],
            dst_ref=precv.at[s, d - 1],
            send_sem=p_ssem.at[s, d - 1],
            recv_sem=p_rsem.at[s, d - 1],
            device_id={"hor": hor + d},
            device_id_type=MESH,
        )

    def rate_copy(d):
        return pltpu.make_async_remote_copy(
            src_ref=ret,
            dst_ref=rrecv.at[d - 1],
            send_sem=r_ssem.at[d - 1],
            recv_sem=r_rsem.at[d - 1],
            device_id={"hor": hor + d},
            device_id_type=MESH,
        )

    def lift(scaled, sm, sh):
        return silu(dot(liftw[...], scaled) * sm + sh).astype(F32)

    def place(feat, block):
        at = block * lon
        low = feat.astype(BF16)
        stack[0:hidden, at : at + lon] = pltpu.roll(feat, 1, 1).astype(BF16)
        stack[hidden : 2 * hidden, at : at + lon] = low
        stack[2 * hidden : 3 * hidden, at : at + lon] = pltpu.roll(feat, lon - 1, 1).astype(BF16)

    loads[0].wait()
    for row in range(rows):
        cur[:, row * lon : (row + 1) * lon] = win[pl.ds(row, chans, stride=rows), :]
    for side in range(2):
        stage_halo(0, side)
    n_near = jnp.where(lat > 0, 1, 0) + jnp.where(lat < n_lat - 1, 1, 0)
    pl.semaphore_wait(barrier, n_near + (n_hor - 1))
    for side in range(2):
        send_halo(0, side)
    for load in loads[1:5]:
        load.wait()
    mods[0] = jnp.broadcast_to(column(msc[...], 0, hidden), (hidden, lon))
    mods[1] = jnp.broadcast_to(column(msh[...], 0, hidden), (hidden, lon))
    eye = (
        lax.broadcasted_iota(jnp.int32, (chans, chans), 0)
        == lax.broadcasted_iota(jnp.int32, (chans, chans), 1)
    ).astype(F32).astype(BF16)
    liftw[...] = lax.dot_general(
        liftt[...], eye, (((0,), (0,)), ((), ())), preferred_element_type=F32
    ).astype(BF16)
    for d in range(1, n_hor):

        @pl.when(hor + d < n_hor)
        def _():
            rate_copy(d).start()

    for load in loads[5:]:
        load.wait()

    @pl.loop(0, STEPS)
    def _(s):
        now, after = sigma(s, lon)
        scale = in_scale_of(now)
        log_sigma = jnp.log(now)
        ratio = after / now
        keep = ratio + (1.0 - ratio) / (now * now + 1.0)
        gain = (1.0 - ratio) * (now * scale)

        @pl.when((s == STEPS - 1) & (hor > 0))
        def _():
            for row in range(rows):
                at = row * lon
                base_send[:, at : at + lon] = keep * cur[:, at : at + lon]
            base_copy.start()

        sm = 1.0 + log_sigma * mods[0]
        sh = log_sigma * mods[1]
        for p in range(n_pairs):
            scaled = jnp.concatenate(
                [
                    (cur[:, (2 * p + i) * lon : (2 * p + i + 1) * lon] * scale).astype(BF16)
                    for i in range(2)
                ],
                axis=1,
            )
            lifted = dot(liftw[...], scaled)
            for i in range(2):
                place(silu(lifted[:, i * lon : (i + 1) * lon] * sm + sh), 2 * p + i + 1)
        pooled = jnp.zeros((half, lon), F32)
        for p in range(n_pairs):
            tok = 2 * p // POOL
            for side in range(2):
                k0 = hidden + side * half
                feat = stack[k0 : k0 + half, (2 * p + 1) * lon : (2 * p + 3) * lon]
                pooled = pooled + dot(feat, poolm[2 * tok + side])
        psend[s] = pooled.astype(WIRE)
        for d in range(1, n_hor):

            @pl.when(hor + d < n_hor)
            def _():
                pool_copy(s, d).start()

        ctx[...] = pooled
        for p in range(n_pairs):
            total = dot(convw[1], stack[:, (2 * p + 1) * lon : (2 * p + 3) * lon])
            if p > 0:
                total = total + dot(convw[0], stack[:, 2 * p * lon : (2 * p + 2) * lon])
            if p < n_pairs - 1:
                total = total + dot(convw[2], stack[:, (2 * p + 2) * lon : (2 * p + 4) * lon])
            acc[:, p * pair : (p + 1) * pair] = total
        acc[:, lon:pair] += dot(convw[0], stack[:, lon:pair])
        last = (rows - 1) * lon
        acc[:, last - lon : last] += dot(convw[2], stack[:, rows * lon : (rows + 1) * lon])

        for side in range(2):

            @pl.when(has(side))
            def _():
                halo_copy(s, 1 - side).wait_recv()

        near = jnp.concatenate([hrecv[s, side, 0:chans, :] for side in range(2)], axis=1)
        near = dot(liftw[...], near)
        for side in range(2):
            feat = silu(near[:, side * lon : (side + 1) * lon] * sm + sh)
            block = 0 if side == 0 else rows + 1
            place(jnp.where(has(side), feat, 0.0), block)
            at = 0 if side == 0 else last
            acc[:, at : at + lon] += dot(
                convw[2 * side], stack[:, block * lon : (block + 1) * lon]
            )

        @pl.when(s == 0)
        def _():
            coef[0] = packed_rate(ret[...])
            for d in range(1, n_hor):

                @pl.when(hor >= d)
                def _():
                    rate_copy(d).wait_recv()
                    if d < n_hor - 1:
                        coef[d] = coef[d - 1] * packed_rate(rrecv[d - 1])

        for d in range(1, n_hor):

            @pl.when(hor >= d)
            def _():
                pool_copy(s, d).wait_recv()
                ctx[...] += coef[d - 1] * precv[s, d - 1].astype(F32)

        total = ctx[...]
        high = total.astype(BF16)
        low = (total - high.astype(F32)).astype(BF16)
        both = jnp.concatenate([high, low], axis=1)
        up[0:half, :] = dot(both, spread[0])
        up[half:hidden, :] = dot(both, spread[1])

        for u, unit in enumerate(units):
            gated = []
            for row in unit:
                at = row * lon
                tok = row // POOL
                ctx_up = up[:, tok * lon : (tok + 1) * lon]
                feat = stack[hidden : 2 * hidden, at + lon : at + 2 * lon].astype(F32)
                gated.append(silu(feat + acc[:, at : at + lon] + ctx_up).astype(BF16))
            gated = gated[0] if len(gated) == 1 else jnp.concatenate(gated, axis=1)
            outputs = dot(outw[...], gated)
            for i, row in enumerate(unit):
                at = row * lon
                step = gain * outputs[:, i * lon : (i + 1) * lon]
                cur[:, at : at + lon] = keep * cur[:, at : at + lon] + step
                gain_send[0:chans, at : at + lon] = step.astype(BF16)
            if u < 2:

                @pl.when(s < STEPS - 1)
                def _():
                    stage_halo(s + 1, u)
                    send_halo(s + 1, u)

            @pl.when((s == STEPS - 1) & (hor > 0))
            def _():
                gain_copy(u).start()

    for row in range(rows):
        wout[pl.ds(row, chans, stride=rows), :] = cur[:, row * lon : (row + 1) * lon]

    @pl.when(hor == n_hor - 1)
    def _():
        fresh_load.wait()
        arr[...] = plan[plan.shape[0] - 1] * arr[...]

    @pl.when(hor < n_hor - 1)
    def _():
        base_copy.wait_recv()
        for u in range(len(units)):
            gain_copy(u).wait_recv()
            for row in units[u]:
                at = row * lon
                arr[pl.ds(row, chans, stride=rows), :] = base_recv[:, at : at + lon] + gain_recv[
                    0:chans, at : at + lon
                ].astype(F32)

    for d in range(1, n_hor):

        @pl.when(hor + d < n_hor)
        def _():
            rate_copy(d).wait_send()
            for s in range(STEPS):
                pool_copy(s, d).wait_send()

    for s in range(STEPS):
        for side in range(2):

            @pl.when(has(side))
            def _():
                halo_copy(s, side).wait_send()

    @pl.when(hor > 0)
    def _():
        base_copy.wait_send()
        for u in range(len(units)):
            gain_copy(u).wait_send()


def write(a, b, a_out, b_out, sem):
    copies = [pltpu.make_async_copy(x, y, sem.at[i]) for i, (x, y) in enumerate([(a, a_out), (b, b_out)])]
    for copy in copies:
        copy.start()
    for copy in copies:
        copy.wait()


def body(
    n_hor,
    n_lat,
    window,
    fresh_noise,
    level_index,
    plan,
    retention,
    lift_weight,
    mod_scale,
    mod_shift,
    conv_weight,
    out_weight,
):
    frames, chans, rows, lon = window.shape
    hidden = conv_weight.shape[1]
    half = hidden // 2
    cells = rows * lon
    cpad = -(-chans // 16) * 16
    peers = max(1, n_hor - 1)
    vmem = pl.BlockSpec(memory_space=pltpu.VMEM)
    hbm = pl.BlockSpec(memory_space=pltpu.HBM)
    smem = pl.BlockSpec(memory_space=pltpu.SMEM)
    flat = jax.ShapeDtypeStruct((chans * rows, lon), F32)
    dma = pltpu.SemaphoreType.DMA
    current, arriving = pl.pallas_call(
        functools.partial(kernel, rows, lon, n_hor, n_lat),
        out_shape=(pltpu.VMEM(flat.shape, F32), pltpu.VMEM(flat.shape, F32)),
        in_specs=[smem, smem] + [hbm] * 8,
        out_specs=(vmem, vmem),
        scratch_shapes=[
            pltpu.VMEM((chans * rows, lon), F32),
            pltpu.VMEM((1, hidden), F32),
            pltpu.VMEM((1, hidden), F32),
            pltpu.VMEM((1, hidden), F32),
            pltpu.VMEM((chans, hidden), BF16),
            pltpu.VMEM(conv_weight.shape, BF16),
            pltpu.VMEM((chans, hidden), BF16),
            pltpu.VMEM((hidden, chans), BF16),
            pltpu.VMEM((chans, cells), F32),
            pltpu.VMEM((chans, cells), F32),
            pltpu.VMEM((cpad, cells), BF16),
            pltpu.VMEM((cpad, cells), BF16),
            pltpu.VMEM((chans, cells), F32),
            pltpu.VMEM((3 * hidden, cells + 2 * lon), BF16),
            pltpu.VMEM((hidden, cells), F32),
            pltpu.VMEM((hidden, 2 * lon), F32),
            pltpu.VMEM((peers, half, lon), F32),
            pltpu.VMEM((2, hidden, lon), F32),
            pltpu.VMEM((2 * (rows // POOL), 2 * lon, lon), BF16),
            pltpu.VMEM((2, 2 * lon, 2 * lon), BF16),
            pltpu.VMEM((half, lon), F32),
            pltpu.VMEM((STEPS, 2, cpad, lon), BF16),
            pltpu.VMEM((STEPS, 2, cpad, lon), BF16),
            pltpu.VMEM((STEPS, half, lon), WIRE),
            pltpu.VMEM((STEPS, peers, half, lon), WIRE),
            pltpu.VMEM((peers, 1, hidden), F32),
            dma((STEPS, 2)),
            dma((STEPS, 2)),
            dma((STEPS, peers)),
            dma((STEPS, peers)),
            dma((peers,)),
            dma((peers,)),
            dma((8,)),
            dma((2,)),
            dma((rows,)),
            dma((rows,)),
        ],
        compiler_params=pltpu.CompilerParams(
            collective_id=0, has_side_effects=True, vmem_limit_bytes=66400000
        ),
    )(
        level_index,
        plan,
        window.reshape(chans * rows, lon),
        fresh_noise.reshape(chans * rows, lon),
        retention,
        mod_scale.reshape(1, hidden),
        mod_shift.reshape(1, hidden),
        lift_weight.T,
        conv_weight,
        out_weight,
    )
    shape = (frames, chans, rows, lon)
    current, rolled = pl.pallas_call(
        write,
        out_shape=(flat, flat),
        in_specs=[vmem, vmem],
        out_specs=(hbm, hbm),
        scratch_shapes=[dma((2,))],
        compiler_params=pltpu.CompilerParams(vmem_limit_bytes=4 * 1024 * 1024),
    )(current, arriving)
    return (current.reshape(shape), rolled.reshape(shape))


def solution(mesh):
    in_specs = (
        P("hor", None, "lat", None),
        P(None, "lat", None),
        P("hor"),
        P(),
        P("hor", None),
        P(),
        P(),
        P(),
        P(),
        P(),
    )
    out_specs = (P("hor", None, "lat", None), P("hor", None, "lat", None))
    run = functools.partial(body, mesh.shape["hor"], mesh.shape["lat"])
    return jax.shard_map(run, mesh=mesh, in_specs=in_specs, out_specs=out_specs, check_vma=False)
```

```python
import functools

import jax
import jax.numpy as jnp
from jax import lax
from jax.experimental import pallas as pl
from jax.experimental.pallas import tpu as pltpu
from jax.sharding import PartitionSpec as P

POOL = 4
STEPS = 3
MESH = pl.DeviceIdType.MESH
F32 = jnp.float32
BF16 = jnp.bfloat16
WIRE = jnp.bfloat16


def dot(a, b):
    return jnp.dot(a, b, preferred_element_type=F32)


def silu(x):
    h = 0.5 * x
    return h + h * jnp.tanh(h)


def kernel(
    rows,
    lon,
    n_hor,
    n_lat,
    lvl,
    plan,
    win_h,
    fresh_h,
    ret_h,
    msc_h,
    msh_h,
    lift_h,
    convw_h,
    outw_h,
    wout,
    arr,
    win,
    ret,
    msc,
    msh,
    liftt,
    convw,
    outw,
    liftw,
    base_send,
    base_recv,
    gain_send,
    gain_recv,
    cur,
    stack,
    acc,
    up,
    coef,
    mods,
    poolm,
    spread,
    ctx,
    hsend,
    hrecv,
    psend,
    precv,
    rrecv,
    h_ssem,
    h_rsem,
    p_ssem,
    p_rsem,
    r_ssem,
    r_rsem,
    l_sem,
    f_sem,
    g_ssem,
    g_rsem,
):
    hidden, chans = liftw.shape
    half = hidden // 2
    pair = 2 * lon
    n_pairs = rows // 2
    hor = lax.axis_index("hor")
    lat = lax.axis_index("lat")

    barrier = pltpu.get_barrier_semaphore()

    @pl.when(lat > 0)
    def _():
        pl.semaphore_signal(barrier, inc=1, device_id={"lat": lat - 1}, device_id_type=MESH)

    @pl.when(lat < n_lat - 1)
    def _():
        pl.semaphore_signal(barrier, inc=1, device_id={"lat": lat + 1}, device_id_type=MESH)

    for d in range(1, n_hor):
        pl.semaphore_signal(
            barrier, inc=1, device_id={"hor": lax.rem(hor + d, n_hor)}, device_id_type=MESH
        )

    pairs = [(win_h, win), (msc_h, msc), (msh_h, msh), (ret_h, ret), (lift_h, liftt)]
    pairs += [(convw_h, convw), (outw_h, outw)]
    loads = [pltpu.make_async_copy(a, b, l_sem.at[i]) for i, (a, b) in enumerate(pairs)]
    fresh_load = pltpu.make_async_copy(fresh_h, arr, l_sem.at[len(pairs)])
    for load in loads:
        load.start()

    @pl.when(hor == n_hor - 1)
    def _():
        fresh_load.start()

    for side in range(2):

        @pl.when(jnp.logical_not(lat > 0 if side == 0 else lat < n_lat - 1))
        def _():
            hrecv[:, side] = jnp.zeros_like(hrecv[:, side])

    def column(row_ref_value, start, count):
        sub = lax.broadcasted_iota(jnp.int32, (count, hidden), 0) + start
        lane = lax.broadcasted_iota(jnp.int32, (count, hidden), 1)
        return jnp.sum(jnp.where(sub == lane, row_ref_value, 0.0), axis=1, keepdims=True)

    def packed_rate(value):
        lane = lax.broadcasted_iota(jnp.int32, (half, lon), 1)
        lo = jnp.broadcast_to(column(value, 0, half), (half, lon))
        hi = jnp.broadcast_to(column(value, half, half), (half, lon))
        return jnp.where(lane < lon // 2, lo, hi)

    groups = lon // POOL
    for tok in range(rows // POOL):
        for side in range(2):
            k = lax.broadcasted_iota(jnp.int32, (pair, lon), 0)
            n = lax.broadcasted_iota(jnp.int32, (pair, lon), 1)
            want = side * (lon // 2) + tok * groups + lax.shift_right_logical(
                lax.bitwise_and(k, lon - 1), POOL.bit_length() - 1
            )
            poolm[2 * tok + side] = jnp.where(want == n, 1.0 / (POOL * POOL), 0.0).astype(BF16)
    for side in range(2):
        k = lax.broadcasted_iota(jnp.int32, (2 * lon, pair), 0)
        n = lax.broadcasted_iota(jnp.int32, (2 * lon, pair), 1)
        want = side * (lon // 2) + lax.shift_right_logical(n, POOL.bit_length() - 1)
        spread[side] = jnp.where(lax.bitwise_and(k, lon - 1) == want, 1.0, 0.0).astype(BF16)

    def sigma(s, width):
        at = lvl[0] - s
        now = jnp.full((1, width), plan[jnp.maximum(at, 0)], F32)
        after = jnp.full((1, width), plan[jnp.maximum(at - 1, 0)], F32)
        return now, after

    def in_scale_of(now):
        return 1.0 / jnp.sqrt(now * now + 1.0)

    def halo_copy(s, side):
        return pltpu.make_async_remote_copy(
            src_ref=hsend.at[s, side],
            dst_ref=hrecv.at[s, 1 - side],
            send_sem=h_ssem.at[s, side],
            recv_sem=h_rsem.at[s, 1 - side],
            device_id={"lat": lat - 1 if side == 0 else lat + 1},
            device_id_type=MESH,
        )

    def has(side):
        return lat > 0 if side == 0 else lat < n_lat - 1

    def stage_halo(s, side):
        scale = in_scale_of(sigma(s, lon)[0])
        at = 0 if side == 0 else (rows - 1) * lon
        hsend[s, side, 0:chans, :] = (cur[:, at : at + lon] * scale).astype(BF16)

    def send_halo(s, side):
        @pl.when(has(side))
        def _():
            halo_copy(s, side).start()

    base_copy = pltpu.make_async_remote_copy(
        src_ref=base_send,
        dst_ref=base_recv,
        send_sem=f_sem.at[0],
        recv_sem=f_sem.at[1],
        device_id={"hor": hor - 1},
        device_id_type=MESH,
    )
    units = [[0], [rows - 1]] + [[r, r + 1] for r in range(1, rows - 1, 2)]

    def gain_copy(u):
        part = pl.ds(units[u][0] * lon, len(units[u]) * lon)
        return pltpu.make_async_remote_copy(
            src_ref=gain_send.at[:, part],
            dst_ref=gain_recv.at[:, part],
            send_sem=g_ssem.at[u],
            recv_sem=g_rsem.at[u],
            device_id={"hor": hor - 1},
            device_id_type=MESH,
        )

    def pool_copy(s, d):
        return pltpu.make_async_remote_copy(
            src_ref=psend.at[s],
            dst_ref=precv.at[s, d - 1],
            send_sem=p_ssem.at[s, d - 1],
            recv_sem=p_rsem.at[s, d - 1],
            device_id={"hor": hor + d},
            device_id_type=MESH,
        )

    def rate_copy(d):
        return pltpu.make_async_remote_copy(
            src_ref=ret,
            dst_ref=rrecv.at[d - 1],
            send_sem=r_ssem.at[d - 1],
            recv_sem=r_rsem.at[d - 1],
            device_id={"hor": hor + d},
            device_id_type=MESH,
        )

    def lift(scaled, sm, sh):
        return silu(dot(liftw[...], scaled) * sm + sh).astype(F32)

    def place(feat, block):
        at = block * lon
        low = feat.astype(BF16)
        stack[0:hidden, at : at + lon] = pltpu.roll(feat, 1, 1).astype(BF16)
        stack[hidden : 2 * hidden, at : at + lon] = low
        stack[2 * hidden : 3 * hidden, at : at + lon] = pltpu.roll(feat, lon - 1, 1).astype(BF16)

    loads[0].wait()
    for row in range(rows):
        cur[:, row * lon : (row + 1) * lon] = win[pl.ds(row, chans, stride=rows), :]
    for side in range(2):
        stage_halo(0, side)
    n_near = jnp.where(lat > 0, 1, 0) + jnp.where(lat < n_lat - 1, 1, 0)
    pl.semaphore_wait(barrier, n_near + (n_hor - 1))
    for side in range(2):
        send_halo(0, side)
    for load in loads[1:5]:
        load.wait()
    mods[0] = jnp.broadcast_to(column(msc[...], 0, hidden), (hidden, lon))
    mods[1] = jnp.broadcast_to(column(msh[...], 0, hidden), (hidden, lon))
    eye = (
        lax.broadcasted_iota(jnp.int32, (chans, chans), 0)
        == lax.broadcasted_iota(jnp.int32, (chans, chans), 1)
    ).astype(F32).astype(BF16)
    liftw[...] = lax.dot_general(
        liftt[...], eye, (((0,), (0,)), ((), ())), preferred_element_type=F32
    ).astype(BF16)
    for d in range(1, n_hor):

        @pl.when(hor + d < n_hor)
        def _():
            rate_copy(d).start()

    for load in loads[5:]:
        load.wait()

    @pl.loop(0, STEPS)
    def _(s):
        now, after = sigma(s, lon)
        scale = in_scale_of(now)
        log_sigma = jnp.log(now)
        ratio = after / now
        keep = ratio + (1.0 - ratio) / (now * now + 1.0)
        gain = (1.0 - ratio) * (now * scale)

        @pl.when((s == STEPS - 1) & (hor > 0))
        def _():
            for row in range(rows):
                at = row * lon
                base_send[:, at : at + lon] = keep * cur[:, at : at + lon]
            base_copy.start()

        sm = 1.0 + log_sigma * mods[0]
        sh = log_sigma * mods[1]
        for p in range(n_pairs):
            scaled = jnp.concatenate(
                [
                    (cur[:, (2 * p + i) * lon : (2 * p + i + 1) * lon] * scale).astype(BF16)
                    for i in range(2)
                ],
                axis=1,
            )
            lifted = dot(liftw[...], scaled)
            for i in range(2):
                place(silu(lifted[:, i * lon : (i + 1) * lon] * sm + sh), 2 * p + i + 1)
        pooled = jnp.zeros((half, lon), F32)
        for p in range(n_pairs):
            tok = 2 * p // POOL
            for side in range(2):
                k0 = hidden + side * half
                feat = stack[k0 : k0 + half, (2 * p + 1) * lon : (2 * p + 3) * lon]
                pooled = pooled + dot(feat, poolm[2 * tok + side])
        psend[s] = pooled.astype(WIRE)
        for d in range(1, n_hor):

            @pl.when(hor + d < n_hor)
            def _():
                pool_copy(s, d).start()

        ctx[...] = pooled
        for p in range(n_pairs):
            total = dot(convw[1], stack[:, (2 * p + 1) * lon : (2 * p + 3) * lon])
            if p > 0:
                total = total + dot(convw[0], stack[:, 2 * p * lon : (2 * p + 2) * lon])
            if p < n_pairs - 1:
                total = total + dot(convw[2], stack[:, (2 * p + 2) * lon : (2 * p + 4) * lon])
            acc[:, p * pair : (p + 1) * pair] = total
        acc[:, lon:pair] += dot(convw[0], stack[:, lon:pair])
        last = (rows - 1) * lon
        acc[:, last - lon : last] += dot(convw[2], stack[:, rows * lon : (rows + 1) * lon])

        @pl.when(s == 0)
        def _():
            coef[0] = packed_rate(ret[...])
            for d in range(1, n_hor):

                @pl.when(hor >= d)
                def _():
                    rate_copy(d).wait_recv()
                    if d < n_hor - 1:
                        coef[d] = coef[d - 1] * packed_rate(rrecv[d - 1])

        for d in range(1, n_hor):

            @pl.when(hor >= d)
            def _():
                pool_copy(s, d).wait_recv()
                ctx[...] += coef[d - 1] * precv[s, d - 1].astype(F32)

        total = ctx[...]
        high = total.astype(BF16)
        low = (total - high.astype(F32)).astype(BF16)
        both = jnp.concatenate([high, low], axis=1)
        up[0:half, :] = dot(both, spread[0])
        up[half:hidden, :] = dot(both, spread[1])

        def finish(u):
            unit = units[u]
            gated = []
            for row in unit:
                at = row * lon
                tok = row // POOL
                ctx_up = up[:, tok * lon : (tok + 1) * lon]
                feat = stack[hidden : 2 * hidden, at + lon : at + 2 * lon].astype(F32)
                gated.append(silu(feat + acc[:, at : at + lon] + ctx_up).astype(BF16))
            gated = gated[0] if len(gated) == 1 else jnp.concatenate(gated, axis=1)
            outputs = dot(outw[...], gated)
            for i, row in enumerate(unit):
                at = row * lon
                step = gain * outputs[:, i * lon : (i + 1) * lon]
                cur[:, at : at + lon] = keep * cur[:, at : at + lon] + step
                gain_send[0:chans, at : at + lon] = step.astype(BF16)
            if u < 2:

                @pl.when(s < STEPS - 1)
                def _():
                    stage_halo(s + 1, u)
                    send_halo(s + 1, u)

            @pl.when((s == STEPS - 1) & (hor > 0))
            def _():
                gain_copy(u).start()

        for u in range(2, len(units)):
            finish(u)

        for side in range(2):

            @pl.when(has(side))
            def _():
                halo_copy(s, 1 - side).wait_recv()

        near = jnp.concatenate([hrecv[s, side, 0:chans, :] for side in range(2)], axis=1)
        near = dot(liftw[...], near)
        for side in range(2):
            feat = silu(near[:, side * lon : (side + 1) * lon] * sm + sh)
            block = 0 if side == 0 else rows + 1
            place(jnp.where(has(side), feat, 0.0), block)
            at = 0 if side == 0 else last
            acc[:, at : at + lon] += dot(
                convw[2 * side], stack[:, block * lon : (block + 1) * lon]
            )

        finish(0)
        finish(1)

    for row in range(rows):
        wout[pl.ds(row, chans, stride=rows), :] = cur[:, row * lon : (row + 1) * lon]

    @pl.when(hor == n_hor - 1)
    def _():
        fresh_load.wait()
        arr[...] = plan[plan.shape[0] - 1] * arr[...]

    @pl.when(hor < n_hor - 1)
    def _():
        base_copy.wait_recv()
        for u in range(len(units)):
            gain_copy(u).wait_recv()
            for row in units[u]:
                at = row * lon
                arr[pl.ds(row, chans, stride=rows), :] = base_recv[:, at : at + lon] + gain_recv[
                    0:chans, at : at + lon
                ].astype(F32)

    for d in range(1, n_hor):

        @pl.when(hor + d < n_hor)
        def _():
            rate_copy(d).wait_send()
            for s in range(STEPS):
                pool_copy(s, d).wait_send()

    for s in range(STEPS):
        for side in range(2):

            @pl.when(has(side))
            def _():
                halo_copy(s, side).wait_send()

    @pl.when(hor > 0)
    def _():
        base_copy.wait_send()
        for u in range(len(units)):
            gain_copy(u).wait_send()


def write(a, b, a_out, b_out, sem):
    copies = [pltpu.make_async_copy(x, y, sem.at[i]) for i, (x, y) in enumerate([(a, a_out), (b, b_out)])]
    for copy in copies:
        copy.start()
    for copy in copies:
        copy.wait()


def body(
    n_hor,
    n_lat,
    window,
    fresh_noise,
    level_index,
    plan,
    retention,
    lift_weight,
    mod_scale,
    mod_shift,
    conv_weight,
    out_weight,
):
    frames, chans, rows, lon = window.shape
    hidden = conv_weight.shape[1]
    half = hidden // 2
    cells = rows * lon
    cpad = -(-chans // 16) * 16
    peers = max(1, n_hor - 1)
    vmem = pl.BlockSpec(memory_space=pltpu.VMEM)
    hbm = pl.BlockSpec(memory_space=pltpu.HBM)
    smem = pl.BlockSpec(memory_space=pltpu.SMEM)
    flat = jax.ShapeDtypeStruct((chans * rows, lon), F32)
    dma = pltpu.SemaphoreType.DMA
    current, arriving = pl.pallas_call(
        functools.partial(kernel, rows, lon, n_hor, n_lat),
        out_shape=(pltpu.VMEM(flat.shape, F32), pltpu.VMEM(flat.shape, F32)),
        in_specs=[smem, smem] + [hbm] * 8,
        out_specs=(vmem, vmem),
        scratch_shapes=[
            pltpu.VMEM((chans * rows, lon), F32),
            pltpu.VMEM((1, hidden), F32),
            pltpu.VMEM((1, hidden), F32),
            pltpu.VMEM((1, hidden), F32),
            pltpu.VMEM((chans, hidden), BF16),
            pltpu.VMEM(conv_weight.shape, BF16),
            pltpu.VMEM((chans, hidden), BF16),
            pltpu.VMEM((hidden, chans), BF16),
            pltpu.VMEM((chans, cells), F32),
            pltpu.VMEM((chans, cells), F32),
            pltpu.VMEM((cpad, cells), BF16),
            pltpu.VMEM((cpad, cells), BF16),
            pltpu.VMEM((chans, cells), F32),
            pltpu.VMEM((3 * hidden, cells + 2 * lon), BF16),
            pltpu.VMEM((hidden, cells), F32),
            pltpu.VMEM((hidden, 2 * lon), F32),
            pltpu.VMEM((peers, half, lon), F32),
            pltpu.VMEM((2, hidden, lon), F32),
            pltpu.VMEM((2 * (rows // POOL), 2 * lon, lon), BF16),
            pltpu.VMEM((2, 2 * lon, 2 * lon), BF16),
            pltpu.VMEM((half, lon), F32),
            pltpu.VMEM((STEPS, 2, cpad, lon), BF16),
            pltpu.VMEM((STEPS, 2, cpad, lon), BF16),
            pltpu.VMEM((STEPS, half, lon), WIRE),
            pltpu.VMEM((STEPS, peers, half, lon), WIRE),
            pltpu.VMEM((peers, 1, hidden), F32),
            dma((STEPS, 2)),
            dma((STEPS, 2)),
            dma((STEPS, peers)),
            dma((STEPS, peers)),
            dma((peers,)),
            dma((peers,)),
            dma((8,)),
            dma((2,)),
            dma((rows,)),
            dma((rows,)),
        ],
        compiler_params=pltpu.CompilerParams(
            collective_id=0, has_side_effects=True, vmem_limit_bytes=66400000
        ),
    )(
        level_index,
        plan,
        window.reshape(chans * rows, lon),
        fresh_noise.reshape(chans * rows, lon),
        retention,
        mod_scale.reshape(1, hidden),
        mod_shift.reshape(1, hidden),
        lift_weight.T,
        conv_weight,
        out_weight,
    )
    shape = (frames, chans, rows, lon)
    current, rolled = pl.pallas_call(
        write,
        out_shape=(flat, flat),
        in_specs=[vmem, vmem],
        out_specs=(hbm, hbm),
        scratch_shapes=[dma((2,))],
        compiler_params=pltpu.CompilerParams(vmem_limit_bytes=4 * 1024 * 1024),
    )(current, arriving)
    return (current.reshape(shape), rolled.reshape(shape))


def solution(mesh):
    in_specs = (
        P("hor", None, "lat", None),
        P(None, "lat", None),
        P("hor"),
        P(),
        P("hor", None),
        P(),
        P(),
        P(),
        P(),
        P(),
    )
    out_specs = (P("hor", None, "lat", None), P("hor", None, "lat", None))
    run = functools.partial(body, mesh.shape["hor"], mesh.shape["lat"])
    return jax.shard_map(run, mesh=mesh, in_specs=in_specs, out_specs=out_specs, check_vma=False)
```
